512 devices in a mesh: dp: 32 (over z, core), vocab: 16 (over y, x).
Axes of the slice: x: 4, y: 4, z: 16, core: 2. Of those that a mesh axis runs over, the one named last changes fastest.
Arguments:
- student_hidden: bfloat16 [192, 5120], P('dp', 'vocab'), may hold values from -71 to 71
- teacher_hidden: bfloat16 [192, 4096], P('dp', 'vocab'), may hold values from -73 to 73
- student_head: bfloat16 [90112, 5120], P(('dp', 'vocab')), may hold values from -16 to 16
- teacher_head: bfloat16 [90112, 4096], P(('dp', 'vocab')), may hold values from -16 to 16
Outputs:
- hidden_grad: bfloat16 [192, 5120], P('dp', 'vocab')
- head_grad: bfloat16 [90112, 5120], P(('dp', 'vocab'))
The draws below stay inside these ranges and needn't reach their ends.
All inputs are finite; a program needn't handle non-finite values.
Results may differ from the reference program's by a relative error of at most 0.017.
Values may be sent and summed in bfloat16 or wider, within the bound.
A program may use at most 64 MiB of HBM per device.

```python
import math
import jax
import jax.numpy as jnp
from jax import lax

D = 5120
DT = 4096
VOC_DEV = 176
VOCAB = 90112
TOKENS = 192
DEVICES = 512


def head_matrix(key, marker, breadth, trended):
    seeded = jax.random.fold_in(key, marker)
    entry_key, scale_key = jax.random.split(seeded)
    rising = 1.0 + 2.0 * jnp.arange(VOCAB, dtype=jnp.float32) / VOCAB
    spread = jnp.exp(jax.random.uniform(scale_key, (VOCAB,), jnp.float32, math.log(0.5), math.log(1.0)))
    if trended:
        trend = rising
    else:
        trend = jnp.ones((VOCAB,), jnp.float32)
    entries = jax.random.normal(entry_key, (VOCAB, breadth), jnp.float32)
    matrix = entries * (spread * trend)[:, None] / math.sqrt(breadth)
    return jnp.clip(matrix, -16.0, 16.0)


def hidden_rows(key, marker, breadth):
    seeded = jax.random.fold_in(key, marker)
    normal_key = jax.random.fold_in(seeded, 0)
    samples = jax.random.normal(normal_key, (TOKENS, breadth), jnp.float32)
    limit = float(64 + 40000 // breadth)
    return jnp.clip(samples, -limit, limit)


def draw_student_head(key, part):
    return head_matrix(key, 11, D, False).astype(jnp.bfloat16)


def draw_teacher_head(key, part):
    return head_matrix(key, 12, DT, True).astype(jnp.bfloat16)


def draw_student_hidden(key, part):
    return hidden_rows(key, 21, D).astype(jnp.bfloat16)


def draw_teacher_hidden(key, part):
    return hidden_rows(key, 22, DT).astype(jnp.bfloat16)


def setup_inputs(seed: int = 0) -> dict:
    key_of = jax.random.split(jax.random.key(seed), 5)
    return {
        "student_hidden": draw_student_hidden(jax.random.fold_in(key_of[4], 71), 0),
        "teacher_hidden": draw_teacher_hidden(jax.random.fold_in(key_of[4], 71), 0),
        "student_head": draw_student_head(jax.random.fold_in(key_of[4], 71), 0),
        "teacher_head": draw_teacher_head(jax.random.fold_in(key_of[4], 71), 0),
    }


def log_total(logits):
    peak = lax.optimization_barrier(jnp.max(logits, axis=1, keepdims=True))
    return peak + jnp.log(lax.optimization_barrier(jnp.sum(jnp.exp(logits - peak), axis=1, keepdims=True)))

def reference(student_hidden, teacher_hidden, student_head, teacher_head):
    student_logits = lax.dot_general(student_hidden, student_head, (((1,), (1,)), ((), ())), preferred_element_type=jnp.float32)
    teacher_logits = lax.dot_general(teacher_hidden, teacher_head, (((1,), (1,)), ((), ())), preferred_element_type=jnp.float32)
    log_student = student_logits - log_total(student_logits)
    log_teacher = teacher_logits - log_total(teacher_logits)
    probs = jnp.exp(log_student)
    gap = log_student - log_teacher
    divergence = lax.optimization_barrier(jnp.sum(probs * gap, axis=1, keepdims=True))
    logit_grad = (probs * (gap - divergence)).astype(jnp.bfloat16)
    hidden_sum = jnp.dot(logit_grad, student_head, preferred_element_type=jnp.float32)
    grad_blocks = jnp.transpose(logit_grad.reshape(TOKENS, DEVICES, VOC_DEV), (1, 0, 2))

    def block_grad(block):
        product = lax.dot_general(block, student_hidden, (((0,), (0,)), ((), ())), preferred_element_type=jnp.float32)
        return product.astype(jnp.bfloat16)
    head_blocks = lax.map(block_grad, grad_blocks)
    head_sum = head_blocks.reshape(VOCAB, D)
    return (hidden_sum.astype(jnp.bfloat16), head_sum)
```

```python
import functools

import jax
import jax.numpy as jnp
from jax import lax
from jax.experimental import pallas as pl
from jax.experimental.pallas import tpu as pltpu
from jax.sharding import PartitionSpec as P

MESH = pl.DeviceIdType.MESH
F32 = jnp.float32
BF16 = jnp.bfloat16
R = 6
FS, FT = 320, 256
WS = 384
W = WS + FT
TP = 128
NEG = ((1,), (1,))


def merge_stats(parts):
    m, s, a, mt, st = (parts[:, i : i + 1, :] for i in range(5))
    top = jnp.max(m, axis=0, keepdims=True)
    top_t = jnp.max(mt, axis=0, keepdims=True)
    w = jnp.exp(m - top)
    total = jnp.sum(w * s, axis=0)
    total_t = jnp.sum(jnp.exp(mt - top_t) * st, axis=0)
    weighted = jnp.sum(w * (a + s * ((m - top) - (mt - top_t))), axis=0)
    zero = jnp.zeros_like(total)
    return jnp.concatenate([top[0], total, weighted, top_t[0], total_t, zero, zero, zero], axis=0)


def kernel(
    Z, Y, X,
    own_ref, sw_hbm, tw_hbm,
    hg_ref, hd_hbm,
    zb, zf, hb, sw, tw, ls, lt, g, sc, sx, sy, sz,
    pown, psend, precv, ps, ra, rb, qa, qb, ra2, rb2, fz, zs, zr, ob,
    wsem, z_s, z_r, a1_s, a1_r, b1_s, b1_r, a2_s, a2_r, b2_s, b2_r, d_s, d_r,
    tc_s, tc_r, tx_s, tx_r, ty_s, ty_r, tz_s, tz_r,
    pc_s, pc_r, ra_s, ra_r, rb_s, rb_r, ra2_s, ra2_r, rb2_s, rb2_r, rz_s, rz_r, osem,
):
    dp, vocab = lax.axis_index("dp"), lax.axis_index("vocab")
    z, c = dp // 2, dp % 2
    y, x = vocab // X, vocab % X
    n = Z * R
    h = n // 2
    QL = X * FS
    NP = Y * X // 2

    def at_z(k):
        return (lax.rem(z + k, Z) * 2 + c, vocab)

    def at_x(k):
        return (dp, y * X + lax.rem(x + k, X))

    def at_y(k):
        return (dp, lax.rem(y + k, Y) * X + x)

    partner = (z * 2 + 1 - c, vocab)

    def copy(src, dst, s, r, dev):
        return pltpu.make_async_remote_copy(
            src_ref=src, dst_ref=dst, send_sem=s, recv_sem=r, device_id=dev, device_id_type=MESH
        )

    w_copy = pltpu.make_async_copy(sw_hbm, sw, wsem.at[0])
    t_copy = pltpu.make_async_copy(tw_hbm, tw, wsem.at[1])
    w_copy.start()
    t_copy.start()

    barrier = pltpu.get_barrier_semaphore()
    for k in range(1, Z):
        pl.semaphore_signal(barrier, inc=1, device_id=at_z(k), device_id_type=MESH)
    for k in range(1, X):
        pl.semaphore_signal(barrier, inc=1, device_id=at_x(k), device_id_type=MESH)
    for k in range(1, Y):
        pl.semaphore_signal(barrier, inc=1, device_id=at_y(k), device_id_type=MESH)
    pl.semaphore_signal(barrier, inc=1, device_id=partner, device_id_type=MESH)
    zb[z] = own_ref[...]
    pl.semaphore_wait(barrier, Z + X + Y - 2)

    zorder = sorted(range(1, Z), key=lambda k: -min(k, Z - k))
    for k in zorder:
        copy(zb.at[z], zb.at[z], z_s.at[k], z_r.at[k], at_z(k)).start()
    for k in reversed(zorder):
        slot = lax.rem(z + Z - k, Z)
        copy(zb.at[slot], zb.at[slot], z_s.at[k], z_r.at[k], at_z(k)).wait_recv()
    for i in range(Z):
        zf[R * i : R * i + R, :] = zb[i, 0:R, :].astype(F32)
    hb[c, y, x] = zf[...].astype(BF16)

    def blk(cc, yy, xx, half):
        return hb.at[cc, yy, xx, pl.ds(half * h, h), :]

    def a1(xx, k):
        return copy(blk(c, y, xx, 0), blk(c, y, xx, 0), a1_s.at[k], a1_r.at[k], at_x(k))

    def b1(yy, k):
        return copy(blk(c, yy, x, 1), blk(c, yy, x, 1), b1_s.at[k], b1_r.at[k], at_y(k))

    def a2(yy, xx, k, i):
        return copy(blk(c, yy, xx, 0), blk(c, yy, xx, 0), a2_s.at[k, i], a2_r.at[k, i], at_y(k))

    def b2(yy, xx, k, i):
        return copy(blk(c, yy, xx, 1), blk(c, yy, xx, 1), b2_s.at[k, i], b2_r.at[k, i], at_x(k))

    def fwd(cc, yy, xx, half):
        return copy(blk(cc, yy, xx, half), blk(cc, yy, xx, half), d_s.at[half, yy, xx], d_r.at[half, yy, xx], partner)

    near_x = sorted(range(1, X), key=lambda k: min(k, X - k))
    near_y = sorted(range(1, Y), key=lambda k: min(k, Y - k))
    for k in reversed(near_x):
        a1(x, k).start()
    for k in reversed(near_y):
        b1(y, k).start()
    for k in reversed(near_y):
        a2(y, x, k, 0).start()
    for k in reversed(near_x):
        b2(y, x, k, 0).start()
    fwd(c, y, x, 0).start()
    fwd(c, y, x, 1).start()
    for k in range(max(X, Y) - 1):
        if k < X - 1:
            i = near_x[k]
            xx = lax.rem(x + X - i, X)
            a1(xx, i).wait_recv()
            for kk in reversed(near_y):
                a2(y, xx, kk, i).start()
            fwd(c, y, xx, 0).start()
        if k < Y - 1:
            i = near_y[k]
            yy = lax.rem(y + Y - i, Y)
            b1(yy, i).wait_recv()
            for kk in reversed(near_x):
                b2(yy, x, kk, i).start()
            fwd(c, yy, x, 1).start()
    order_x = [0] + near_x
    order_y = [0] + near_y
    for i in order_x:
        for k in near_y:
            yy, xx = lax.rem(y + Y - k, Y), lax.rem(x + X - i, X)
            a2(yy, xx, k, i).wait_recv()
            fwd(c, yy, xx, 0).start()
    for i in order_y:
        for k in near_x:
            yy, xx = lax.rem(y + Y - i, Y), lax.rem(x + X - k, X)
            b2(yy, xx, k, i).wait_recv()
            fwd(c, yy, xx, 1).start()

    def each_block(fn):
        @pl.loop(0, Y)
        def _(yy):
            @pl.loop(0, X)
            def _(xx):
                fn(yy, xx, 0)
                fn(yy, xx, 1)

    each_block(lambda yy, xx, half: fwd(1 - c, yy, xx, half).wait_recv())
    w_copy.wait()
    t_copy.wait()

    fill = TP - n
    pairs_y = X // 2

    def pair(p):
        yy, xx = p // pairs_y, (p % pairs_y) * 2
        s, t = [], []
        for cc in range(2):
            even, odd = hb[cc, yy, xx], hb[cc, yy, xx + 1]
            s.append(
                jnp.concatenate([even[:, :256], even[:, 256:384] + odd[:, :128], odd[:, 128:384]], axis=1)
            )
            t.append(jnp.concatenate([even[:, 384:], odd[:, 384:]], axis=1))
            s.append(jnp.zeros((fill, 2 * FS), BF16))
            t.append(jnp.zeros((fill, 2 * FT), BF16))
        return jnp.concatenate(s, axis=0), jnp.concatenate(t, axis=0)

    ls[...] = jnp.zeros_like(ls)
    lt[...] = jnp.zeros_like(lt)

    @pl.loop(0, NP)
    def _(p):
        s, t = pair(p)
        at_s = pl.ds(pl.multiple_of(p * (2 * FS), 128), 2 * FS)
        at_t = pl.ds(pl.multiple_of(p * (2 * FT), 128), 2 * FT)
        ls[...] += lax.dot_general(sw[:, at_s], s, (NEG, ((), ())), preferred_element_type=F32)
        lt[...] += lax.dot_general(tw[:, at_t], t, (NEG, ((), ())), preferred_element_type=F32)

    m = jnp.max(ls[...], axis=0, keepdims=True)
    mt = jnp.max(lt[...], axis=0, keepdims=True)
    ds, dt = ls[...] - m, lt[...] - mt
    e = jnp.exp(ds)
    zero = jnp.zeros_like(m)
    sc[c] = jnp.concatenate(
        [
            m,
            jnp.sum(e, axis=0, keepdims=True),
            jnp.sum(e * (ds - dt), axis=0, keepdims=True),
            mt,
            jnp.sum(jnp.exp(dt), axis=0, keepdims=True),
            zero, zero, zero,
        ],
        axis=0,
    )
    copy(sc.at[c], sc.at[c], tc_s, tc_r, partner).start()
    copy(sc.at[1 - c], sc.at[1 - c], tc_s, tc_r, partner).wait_recv()
    sx[x] = merge_stats(sc[...])
    for k in reversed(near_x):
        copy(sx.at[x], sx.at[x], tx_s.at[k], tx_r.at[k], at_x(k)).start()
    for k in near_x:
        slot = lax.rem(x + X - k, X)
        copy(sx.at[slot], sx.at[slot], tx_s.at[k], tx_r.at[k], at_x(k)).wait_recv()
    sy[y] = merge_stats(sx[...])
    for k in reversed(near_y):
        copy(sy.at[y], sy.at[y], ty_s.at[k], ty_r.at[k], at_y(k)).start()
    for k in near_y:
        slot = lax.rem(y + Y - k, Y)
        copy(sy.at[slot], sy.at[slot], ty_s.at[k], ty_r.at[k], at_y(k)).wait_recv()
    sz[z] = merge_stats(sy[...])
    for k in zorder:
        copy(sz.at[z], sz.at[z], tz_s.at[k], tz_r.at[k], at_z(k)).start()
    for k in reversed(zorder):
        slot = lax.rem(z + Z - k, Z)
        copy(sz.at[slot], sz.at[slot], tz_s.at[k], tz_r.at[k], at_z(k)).wait_recv()
    st = merge_stats(sz[...])

    top, total, weighted, top_t, total_t = (st[i : i + 1] for i in range(5))
    log_total, log_total_t = jnp.log(total), jnp.log(total_t)
    divergence = weighted / total - log_total + log_total_t
    log_student = (ls[...] - top) - log_total
    log_teacher = (lt[...] - top_t) - log_total_t
    grad = jnp.exp(log_student) * ((log_student - log_teacher) - divergence)
    lane = lax.broadcasted_iota(jnp.int32, grad.shape, 1)
    grad = jnp.where(lane % TP < n, grad, 0.0).astype(BF16)
    g[...] = grad

    @pl.loop(0, Y)
    def _(i):
        yy = lax.rem(y + 1 + i, Y)

        @pl.loop(0, pairs_y)
        def _(q):
            at_s = pl.ds(pl.multiple_of(yy * QL + q * (2 * FS), 128), 2 * FS)
            rows = lax.dot_general(g[...], sw[:, at_s], (((0,), (0,)), ((), ())), preferred_element_type=F32)
            at_q = pl.ds(pl.multiple_of(q * (2 * FS), 128), 2 * FS)
            lo, hi = rows[0:n], rows[TP : TP + n]
            pown[yy, :, at_q] = jnp.where(c == 0, lo, hi)
            psend[yy, :, at_q] = jnp.where(c == 0, hi, lo).astype(BF16)

        copy(psend.at[yy], precv.at[yy], pc_s.at[yy], pc_r.at[yy], partner).start()

    def win(xx):
        return pl.multiple_of((5 * xx // 2) * 128, 128)

    @pl.loop(0, Y)
    def _(i):
        yy = lax.rem(y + 1 + i, Y)
        copy(psend.at[yy], precv.at[yy], pc_s.at[yy], pc_r.at[yy], partner).wait_recv()
        ps[yy] = (pown[yy] + precv[yy].astype(F32)).astype(BF16)
        for k in reversed(near_x):
            src = ps.at[yy, pl.ds(0, h), pl.ds(win(lax.rem(x + k, X)), WS)]
            copy(src, ra.at[k, yy], ra_s.at[k, yy], ra_r.at[k, yy], at_x(k)).start()

        @pl.when(i < Y - 1)
        def _():
            k = i + 1
            copy(ps.at[yy, pl.ds(h, h), :], rb.at[k], rb_s.at[k], rb_r.at[k], at_y(k)).start()

    @pl.loop(0, NP)
    def _(p):
        s, _t = pair(p)
        at_s = pl.ds(pl.multiple_of(p * (2 * FS), 128), 2 * FS)
        ob[:, at_s] = jnp.dot(g[...], s, preferred_element_type=F32).astype(BF16)
        pltpu.make_async_copy(ob.at[:, at_s], hd_hbm.at[:, at_s], osem.at[p]).start()

    def ra_copy(k, yy):
        return copy(ra.at[k, yy], ra.at[k, yy], ra_s.at[k, yy], ra_r.at[k, yy], at_x(k))

    def rb_copy(k):
        return copy(rb.at[k], rb.at[k], rb_s.at[k], rb_r.at[k], at_y(k))

    for k in near_x:
        @pl.loop(0, Y)
        def _(yy):
            ra_copy(k, yy).wait_recv()

    @pl.loop(0, Y)
    def _(i):
        yy = lax.rem(y + 1 + i, Y)
        acc = ps[yy, 0:h, pl.ds(win(x), WS)].astype(F32)
        for k in range(1, X):
            acc += ra[k, yy].astype(F32)
        qa[yy] = acc.astype(BF16)

        @pl.when(i < Y - 1)
        def _():
            k = i + 1
            copy(qa.at[yy], ra2.at[k], ra2_s.at[k], ra2_r.at[k], at_y(k)).start()

    for k in near_y:
        rb_copy(k).wait_recv()
    acc = ps[y, h : 2 * h, :].astype(F32)
    for k in range(1, Y):
        acc += rb[k].astype(F32)
    qb[...] = acc.astype(BF16)

    def rb2_copy(k):
        src = qb.at[:, pl.ds(win(lax.rem(x + k, X)), WS)]
        return copy(src, rb2.at[k], rb2_s.at[k], rb2_r.at[k], at_x(k))

    def ra2_copy(k):
        return copy(ra2.at[k], ra2.at[k], ra2_s.at[k], ra2_r.at[k], at_y(k))

    for k in reversed(near_x):
        rb2_copy(k).start()
    for k in near_y:
        ra2_copy(k).wait_recv()
    acc = qa[y].astype(F32)
    for k in range(1, Y):
        acc += ra2[k].astype(F32)
    fz[0:h] = acc
    for k in near_x:
        rb2_copy(k).wait_recv()
    acc = qb[:, pl.ds(win(x), WS)].astype(F32)
    for k in range(1, X):
        acc += rb2[k].astype(F32)
    fz[h : 2 * h] = acc

    for i in range(Z):
        zs[i, 0:R, :] = fz[R * i : R * i + R, :].astype(BF16)
        zs[i, R:8, :] = jnp.zeros((8 - R, WS), BF16)
    for k in zorder:
        copy(zs.at[lax.rem(z + k, Z)], zr.at[k], rz_s.at[k], rz_r.at[k], at_z(k)).start()
    for k in reversed(zorder):
        copy(zs.at[lax.rem(z + k, Z)], zr.at[k], rz_s.at[k], rz_r.at[k], at_z(k)).wait_recv()
    acc = zs[z].astype(F32)
    for k in range(1, Z):
        acc += zr[k].astype(F32)
    hg_ref[...] = acc.astype(BF16)

    for k in zorder:
        copy(zb.at[z], zb.at[z], z_s.at[k], z_r.at[k], at_z(k)).wait_send()
        copy(sz.at[z], sz.at[z], tz_s.at[k], tz_r.at[k], at_z(k)).wait_send()
        copy(zs.at[0], zr.at[k], rz_s.at[k], rz_r.at[k], at_z(k)).wait_send()
    for k in near_x:
        a1(x, k).wait_send()
        copy(sx.at[x], sx.at[x], tx_s.at[k], tx_r.at[k], at_x(k)).wait_send()
        rb2_copy(k).wait_send()
        for i in order_y:
            b2(lax.rem(y + Y - i, Y), x, k, i).wait_send()

        @pl.loop(0, Y)
        def _(yy):
            ra_copy(k, yy).wait_send()

    for k in near_y:
        b1(y, k).wait_send()
        copy(sy.at[y], sy.at[y], ty_s.at[k], ty_r.at[k], at_y(k)).wait_send()
        ra2_copy(k).wait_send()
        rb_copy(k).wait_send()
        for i in order_x:
            a2(y, lax.rem(x + X - i, X), k, i).wait_send()
    each_block(lambda yy, xx, half: fwd(c, yy, xx, half).wait_send())
    copy(sc.at[c], sc.at[c], tc_s, tc_r, partner).wait_send()

    @pl.loop(0, Y)
    def _(yy):
        copy(psend.at[yy], precv.at[yy], pc_s.at[yy], pc_r.at[yy], partner).wait_send()

    @pl.loop(0, NP)
    def _(p):
        at_s = pl.ds(pl.multiple_of(p * (2 * FS), 128), 2 * FS)
        pltpu.make_async_copy(ob.at[:, at_s], hd_hbm.at[:, at_s], osem.at[p]).wait()


def build(mesh, Z, Y, X):
    def on_device(sh, th, sw, tw):
        n = Z * R
        h = n // 2
        V, D = sw.shape
        DT = tw.shape[1]
        QL = X * FS
        odd = lax.axis_index("vocab") % 2 == 1
        rows = ((0, 8 - R),)
        stud = jnp.where(
            odd, jnp.pad(sh, rows + ((WS - FS, 0),)), jnp.pad(sh, rows + ((0, WS - FS),))
        )
        own = jnp.concatenate([stud, jnp.pad(th, rows + ((0, 0),))], axis=1)
        V2 = lambda s, d: pltpu.VMEM(s, d)
        DMA = pltpu.SemaphoreType.DMA
        scratch = [
            V2((Z, 8, W), BF16),
            V2((n, W), F32),
            V2((2, Y, X, n, W), BF16),
            V2((V, D), BF16),
            V2((V, DT), BF16),
            V2((V, 2 * TP), F32),
            V2((V, 2 * TP), F32),
            V2((V, 2 * TP), BF16),
            V2((2, 8, 2 * TP), F32),
            V2((X, 8, 2 * TP), F32),
            V2((Y, 8, 2 * TP), F32),
            V2((Z, 8, 2 * TP), F32),
            V2((Y, n, QL), F32),
            V2((Y, n, QL), BF16),
            V2((Y, n, QL), BF16),
            V2((Y, n, QL), BF16),
            V2((X, Y, h, WS), BF16),
            V2((Y, h, QL), BF16),
            V2((Y, h, WS), BF16),
            V2((h, QL), BF16),
            V2((Y, h, WS), BF16),
            V2((X, h, WS), BF16),
            V2((n, WS), F32),
            V2((Z, 8, WS), BF16),
            V2((Z, 8, WS), BF16),
            V2((V, D), BF16),
            DMA((2,)),
            DMA((Z,)), DMA((Z,)),
            DMA((X,)), DMA((X,)), DMA((Y,)), DMA((Y,)),
            DMA((Y, X)), DMA((Y, X)), DMA((X, Y)), DMA((X, Y)),
            DMA((2, Y, X)), DMA((2, Y, X)),
            DMA, DMA, DMA((X,)), DMA((X,)), DMA((Y,)), DMA((Y,)), DMA((Z,)), DMA((Z,)),
            DMA((Y,)), DMA((Y,)),
            DMA((X, Y)), DMA((X, Y)), DMA((Y,)), DMA((Y,)),
            DMA((Y,)), DMA((Y,)), DMA((X,)), DMA((X,)),
            DMA((Z,)), DMA((Z,)), DMA((Y * X // 2,)),
        ]
        hg, hd = pl.pallas_call(
            functools.partial(kernel, Z, Y, X),
            out_shape=(
                jax.ShapeDtypeStruct((8, WS), BF16),
                jax.ShapeDtypeStruct((V, D), BF16),
            ),
            in_specs=[
                pl.BlockSpec(memory_space=pltpu.VMEM),
                pl.BlockSpec(memory_space=pl.ANY),
                pl.BlockSpec(memory_space=pl.ANY),
            ],
            out_specs=(pl.BlockSpec(memory_space=pltpu.VMEM), pl.BlockSpec(memory_space=pl.ANY)),
            scratch_shapes=scratch,
            compiler_params=pltpu.CompilerParams(
                collective_id=0, has_side_effects=True, vmem_limit_bytes=56 << 20
            ),
        )(own, sw, tw)
        hg = jnp.where(odd, hg[:R, WS - FS :], hg[:R, :FS])
        return hg, hd

    return jax.shard_map(
        on_device,
        mesh=mesh,
        in_specs=(
            P("dp", "vocab"),
            P("dp", "vocab"),
            P(("dp", "vocab"), None),
            P(("dp", "vocab"), None),
        ),
        out_specs=(P("dp", "vocab"), P(("dp", "vocab"), None)),
        check_vma=False,
    )


def solution(mesh):
    return build(mesh, mesh.shape["dp"] // 2, 4, mesh.shape["vocab"] // 4)
```
